32 devices in a mesh: dp: 8 (over z, x), sect: 4 (over y, core).
Axes of the slice: x: 2, y: 2, z: 4, core: 2. Of those that a mesh axis runs over, the one named last changes fastest.
Arguments:
- queries: bfloat16 [8, 16, 8192], P('dp', None, 'sect'), may hold values from -5 to 5
- keys: bfloat16 [8, 16, 8192], P('dp', None, 'sect'), may hold values from -5 to 5
- values: bfloat16 [8, 16, 8192], P('dp', None, 'sect'), may hold values from -6 to 6
- residual: bfloat16 [8, 16, 8192], P('dp'), may hold values from -6 to 6
- labels: int32 [8, 16], P('dp'), may hold values from 0 to 2, as said below
- slot_modality: int32 [4], replicated, may hold values from 0 to 2, as said below
- gains: float32 [3, 8192], replicated, may hold values from 0.1 to 1.9
- up_weight: bfloat16 [4, 11008, 8192], P('sect', 'dp'), may hold values from -0.0625 to 0.0625
- down_weight: bfloat16 [4, 11008, 8192], P('sect', 'dp'), may hold values from -0.0546875 to 0.0546875
- cotangent: bfloat16 [8, 16, 8192], P('dp'), may hold values from -6 to 6
Outputs:
- output: bfloat16 [8, 16, 8192], P('dp', 'sect')
- residual_grad: bfloat16 [8, 16, 8192], P('dp', 'sect')
- query_grad: bfloat16 [8, 16, 8192], P('dp', None, 'sect')
- key_grad: bfloat16 [8, 16, 8192], P('dp', None, 'sect')
- value_grad: bfloat16 [8, 16, 8192], P('dp', None, 'sect')
- up_grad: bfloat16 [4, 11008, 8192], P('sect', 'dp')
- down_grad: bfloat16 [4, 11008, 8192], P('sect', 'dp')
- gain_grad: float32 [3, 8192], replicated
The draws below stay inside these ranges and needn't reach their ends.
Inputs may be any that keep to these rules, and one draw needn't show every extreme that they name: `labels`: every sequence holds exactly 8 text tokens (label 0); its other tokens are image or speech. `slot_modality`: text owns two slots, image one, speech one.
All inputs are finite; a program needn't handle non-finite values.
Results may differ from the reference program's by a relative error of at most 0.015.
The reference program's roundings to bfloat16 on the way count: a program that leaves them out, or rounds other values in their place, can miss the bound.
Values may be sent and summed in bfloat16 or wider, within the bound.
A program may use at most 192 MiB of HBM per device.

```python
import jax
import jax.numpy as jnp
from jax import lax

D = 8192
HD = 128
FH = 11008
MODALITIES = 3
L = 16
SEQS = 8
N_SECT = 4


def attention_pair(key):
    base_key = jax.random.fold_in(key, 7)
    first, second = jax.random.split(base_key, 2)
    shape = (SEQS, L, D)
    key_vals = jnp.clip(jax.random.normal(first, shape, jnp.float32), -5.0, 5.0)
    query_vals = jnp.clip(jax.random.normal(second, shape, jnp.float32), -5.0, 5.0)
    return (query_vals, key_vals)


def draw_queries(key, part):
    return attention_pair(key)[0].astype(jnp.bfloat16)


def draw_keys(key, part):
    return attention_pair(key)[1].astype(jnp.bfloat16)


def draw_labels(key, part):
    seq_keys = jax.random.split(jax.random.fold_in(key, 3), SEQS)
    orders = jax.vmap(lambda one_key: jax.random.permutation(one_key, L))(seq_keys)
    others = jax.random.randint(jax.random.fold_in(key, 5), (SEQS, L), 1, 3)
    return jnp.where(orders < L // 2, 0, others).astype(jnp.int32)


def draw_slot_modality(key, part):
    order = jax.random.permutation(jax.random.fold_in(key, 9), 4)
    table = jnp.array([0, 0, 1, 2], jnp.int32)
    return jnp.take(table, order).astype(jnp.int32)


def block_levels(own_key, shape, pieces, smallest, high):
    loudness, own = 1.0, jax.random.fold_in(own_key, 6)
    for dim, parts in pieces:
        draws = jnp.exp(jax.random.uniform(jax.random.fold_in(own, dim), (parts,), jnp.float32, smallest / len(pieces), high / len(pieces)))
        loudness = loudness * jnp.repeat(draws, shape[dim] // parts).reshape([-1 if axis == dim else 1 for axis in range(len(shape))])
    return loudness


def centred(key, dims, deviation, bound, pieces=(), dtype=jnp.bfloat16):
    values = deviation * jax.random.normal(key, dims, jnp.float32)
    if pieces:
        values = values * block_levels(key, dims, pieces, -0.22, 0.18)
    return jnp.clip(values, -bound, bound).astype(dtype)


def setup_inputs(seed: int = 0) -> dict:
    key_of = jax.random.split(jax.random.key(seed), 11)
    queries = draw_queries(jax.random.fold_in(key_of[10], 71), 0)
    keys = draw_keys(jax.random.fold_in(key_of[10], 71), 0)
    values = centred(key_of[2], (SEQS, L, D), 1.0, 6.0, ((0, 8), (2, 4)))
    residual = centred(key_of[3], (SEQS, L, D), 1.0, 6.0, ((0, 8),))
    labels = draw_labels(jax.random.fold_in(key_of[10], 71), 0)
    slot_modality = draw_slot_modality(jax.random.fold_in(key_of[10], 71), 0)
    gains = jnp.clip(1.0 + 0.18 * jax.random.normal(key_of[6], (MODALITIES, D), jnp.float32), 0.1, 1.9)
    up_weight = centred(key_of[7], (N_SECT, FH, D), D ** -0.5, 0.0625, ((0, 4), (1, 8)))
    down_weight = centred(key_of[8], (N_SECT, FH, D), FH ** -0.5, 0.0546875, ((0, 4), (1, 8)))
    cotangent = centred(key_of[9], (SEQS, L, D), 1.0, 6.0, ((0, 8),))
    return {"queries": queries, "keys": keys, "values": values, "residual": residual, "labels": labels, "slot_modality": slot_modality, "gains": gains, "up_weight": up_weight, "down_weight": down_weight, "cotangent": cotangent}


def causal_forward(queries, keys, values):
    seq_count, length, width = queries.shape
    head_count = width // HD
    query_f = queries.astype(jnp.float32).reshape(seq_count, length, head_count, HD)
    key_f = keys.astype(jnp.float32).reshape(seq_count, length, head_count, HD)
    value_f = values.astype(jnp.float32).reshape(seq_count, length, head_count, HD)
    scores = jnp.einsum('sqhd,skhd->shqk', query_f, key_f) * HD ** (-0.5)
    position = jnp.arange(length)
    causal = position[:, None] >= position[None, :]
    scores = jnp.where(causal, scores, -1e+30)
    probs = jax.nn.softmax(scores, axis=-1)
    probs_b = probs.astype(jnp.bfloat16)
    attended = jnp.einsum('shqk,skhd->sqhd', probs_b.astype(jnp.float32), value_f)
    return (attended.astype(jnp.bfloat16).reshape(seq_count, length, width), probs, probs_b)

def causal_backward(grad_out, queries, keys, values, attended, probs, probs_b):
    seq_count, length, width = queries.shape
    head_count = width // HD
    shape = (seq_count, length, head_count, HD)
    grad_f = grad_out.astype(jnp.float32).reshape(shape)
    query_f = queries.astype(jnp.float32).reshape(shape)
    key_f = keys.astype(jnp.float32).reshape(shape)
    value_f = values.astype(jnp.float32).reshape(shape)
    attended_f = attended.astype(jnp.float32).reshape(shape)
    value_grad = jnp.einsum('shqk,sqhd->skhd', probs_b.astype(jnp.float32), grad_f).astype(jnp.bfloat16)
    dprob = jnp.einsum('sqhd,skhd->shqk', grad_f, value_f)
    delta = jnp.einsum('sqhd,sqhd->shq', grad_f, attended_f)
    dscore = (probs * (dprob - delta[..., None]) * HD ** (-0.5)).astype(jnp.bfloat16).astype(jnp.float32)
    query_grad = jnp.einsum('shqk,skhd->sqhd', dscore, key_f).astype(jnp.bfloat16)
    key_grad = jnp.einsum('shqk,sqhd->skhd', dscore, query_f).astype(jnp.bfloat16)
    return (query_grad.reshape(seq_count, length, width), key_grad.reshape(seq_count, length, width), value_grad.reshape(seq_count, length, width))

def block_sum(left, weight):
    return jnp.dot(left, weight, preferred_element_type=jnp.float32)

def reference(queries, keys, values, residual, labels, slot_modality, gains, up_weight, down_weight, cotangent):
    attended, probs, probs_b = causal_forward(queries, keys, values)
    hidden = (residual.astype(jnp.float32) + attended.astype(jnp.float32)).astype(jnp.bfloat16)
    hidden_f = hidden.astype(jnp.float32).reshape(-1, D)
    token_labels = labels.reshape(-1)
    onehot = (token_labels[:, None] == jnp.arange(MODALITIES)[None, :]).astype(jnp.float32)
    gain_rows = gains[token_labels]
    inverse = lax.rsqrt(lax.optimization_barrier(jnp.mean(hidden_f * hidden_f, axis=-1, keepdims=True)) + 1e-05)
    normed_f = hidden_f * inverse
    normed = (normed_f * gain_rows).astype(jnp.bfloat16)
    grad_rows = cotangent.reshape(-1, D)
    ffn = jnp.zeros(hidden_f.shape, jnp.float32)
    norm_grad = jnp.zeros(hidden_f.shape, jnp.float32)
    up_grads = []
    down_grads = []
    for slot_number in range(N_SECT):
        keep_mask = (token_labels == slot_modality[slot_number])[:, None]
        slot_rows = jnp.where(keep_mask, normed, jnp.zeros((), jnp.bfloat16))
        slot_cot = jnp.where(keep_mask, grad_rows, jnp.zeros((), jnp.bfloat16))
        preact = jnp.dot(slot_rows, up_weight[slot_number].T, preferred_element_type=jnp.float32)
        activated = jax.nn.silu(preact).astype(jnp.bfloat16)
        ffn = ffn + block_sum(activated, down_weight[slot_number])
        back = jnp.dot(slot_cot, down_weight[slot_number].T, preferred_element_type=jnp.float32)
        sigma = jax.nn.sigmoid(preact)
        pre_grad = (back * sigma * (1.0 + preact * (1.0 - sigma))).astype(jnp.bfloat16)
        down_grads.append(jnp.dot(activated.T, slot_cot, preferred_element_type=jnp.float32).astype(jnp.bfloat16))
        up_grads.append(jnp.dot(pre_grad.T, slot_rows, preferred_element_type=jnp.float32).astype(jnp.bfloat16))
        norm_grad = norm_grad + block_sum(pre_grad, up_weight[slot_number])
    output = (hidden_f + ffn).astype(jnp.bfloat16).reshape(residual.shape)
    scaled = norm_grad * gain_rows
    hidden_grad = grad_rows.astype(jnp.float32) + inverse * (scaled - normed_f * lax.optimization_barrier(jnp.mean(scaled * normed_f, axis=-1, keepdims=True)))
    residual_grad = hidden_grad.astype(jnp.bfloat16).reshape(residual.shape)
    gain_grad = jnp.dot(onehot.T, norm_grad * normed_f, precision=lax.Precision.HIGHEST)
    query_grad, key_grad, value_grad = causal_backward(residual_grad, queries, keys, values, attended, probs, probs_b)
    return (output, residual_grad, query_grad, key_grad, value_grad, jnp.stack(up_grads), jnp.stack(down_grads), gain_grad)
```

```python
import functools

import jax
import jax.numpy as jnp
from jax import lax
from jax.experimental import pallas as pl
from jax.experimental.pallas import tpu as pltpu
from jax.sharding import PartitionSpec as P

HD = 128
MODALITIES = 3


def causal_forward(queries, keys, values):
    seq_count, length, width = queries.shape
    head_count = width // HD
    query_f = queries.astype(jnp.float32).reshape(seq_count, length, head_count, HD)
    key_f = keys.astype(jnp.float32).reshape(seq_count, length, head_count, HD)
    value_f = values.astype(jnp.float32).reshape(seq_count, length, head_count, HD)
    scores = jnp.einsum("sqhd,skhd->shqk", query_f, key_f) * HD ** (-0.5)
    position = jnp.arange(length)
    causal = position[:, None] >= position[None, :]
    scores = jnp.where(causal, scores, -1e30)
    probs = jax.nn.softmax(scores, axis=-1)
    probs_b = probs.astype(jnp.bfloat16)
    attended = jnp.einsum("shqk,skhd->sqhd", probs_b.astype(jnp.float32), value_f)
    return (attended.astype(jnp.bfloat16).reshape(seq_count, length, width), probs, probs_b)


def causal_backward(grad_out, queries, keys, values, attended, probs, probs_b):
    seq_count, length, width = queries.shape
    head_count = width // HD
    shape = (seq_count, length, head_count, HD)
    grad_f = grad_out.astype(jnp.float32).reshape(shape)
    query_f = queries.astype(jnp.float32).reshape(shape)
    key_f = keys.astype(jnp.float32).reshape(shape)
    value_f = values.astype(jnp.float32).reshape(shape)
    attended_f = attended.astype(jnp.float32).reshape(shape)
    value_grad = jnp.einsum("shqk,sqhd->skhd", probs_b.astype(jnp.float32), grad_f).astype(
        jnp.bfloat16
    )
    dprob = jnp.einsum("sqhd,skhd->shqk", grad_f, value_f)
    delta = jnp.einsum("sqhd,sqhd->shq", grad_f, attended_f)
    dscore = (
        (probs * (dprob - delta[..., None]) * HD ** (-0.5)).astype(jnp.bfloat16).astype(jnp.float32)
    )
    query_grad = jnp.einsum("shqk,skhd->sqhd", dscore, key_f).astype(jnp.bfloat16)
    key_grad = jnp.einsum("shqk,sqhd->skhd", dscore, query_f).astype(jnp.bfloat16)
    return (
        query_grad.reshape(seq_count, length, width),
        key_grad.reshape(seq_count, length, width),
        value_grad.reshape(seq_count, length, width),
    )


MESH = pl.DeviceIdType.MESH
VMEM_BYTES = 60 * 1024 * 1024


def remote(src, dst, send_sem, recv_sem, dp_index, sect_index):
    return pltpu.make_async_remote_copy(
        src_ref=src,
        dst_ref=dst,
        send_sem=send_sem,
        recv_sem=recv_sem,
        device_id=(dp_index, sect_index),
        device_id_type=MESH,
    )


def greet(peers):
    barrier = pltpu.get_barrier_semaphore()
    total = jnp.int32(0)
    for dp_index, sect_index, present in peers:
        if present is None:
            pl.semaphore_signal(barrier, inc=1, device_id=(dp_index, sect_index), device_id_type=MESH)
            total = total + 1
        else:

            @pl.when(present)
            def _():
                pl.semaphore_signal(
                    barrier, inc=1, device_id=(dp_index, sect_index), device_id_type=MESH
                )

            total = total + present.astype(jnp.int32)
    pl.semaphore_wait(barrier, total)


class LineGather:
    def __init__(self, buf, sems, lines, slot):
        self.buf, self.lines = buf, lines
        self.send_sems, self.recv_sems = sems
        self.slot = slot
        self.me = lax.axis_index("dp")
        self.sect = lax.axis_index("sect")
        self.outer, self.inner = self.me // 2, self.me % 2

    def copy(self, way, outer, target, incoming=False):
        inner = (1 - self.inner) if (incoming and way == 2) else self.inner
        block = self.buf.at[outer * 2 + inner]
        recv = 1 if way == 2 else 0
        return remote(
            block,
            block,
            self.send_sems.at[self.slot, way, outer],
            self.recv_sems.at[self.slot, recv, outer],
            target,
            self.sect,
        )

    def pass_up(self, outer):
        return self.copy(0, outer, jnp.minimum(self.outer + 1, self.lines - 1) * 2 + self.inner)

    def pass_down(self, outer):
        return self.copy(1, outer, jnp.maximum(self.outer - 1, 0) * 2 + self.inner)

    def pass_across(self, outer):
        return self.copy(2, outer, self.outer * 2 + 1 - self.inner)

    def start(self):
        outer = self.outer

        @pl.when(outer + 1 < self.lines)
        def _():
            self.pass_up(outer).start()

        @pl.when(outer > 0)
        def _():
            self.pass_down(outer).start()

        self.pass_across(outer).start()

    def relay(self, step):
        outer = self.outer

        @pl.when(outer - step >= 0)
        def _():
            block = outer - step
            self.pass_down(block).wait_recv()

            @pl.when(outer + 1 < self.lines)
            def _():
                self.pass_up(block).start()

            self.pass_across(block).start()

        @pl.when(outer + step < self.lines)
        def _():
            block = outer + step
            self.pass_up(block).wait_recv()

            @pl.when(outer > 0)
            def _():
                self.pass_down(block).start()

            self.pass_across(block).start()

    def finish(self):
        outer = self.outer
        for block in range(self.lines):
            self.copy(2, block, self.outer * 2 + 1 - self.inner, incoming=True).wait_recv()
            self.pass_across(block).wait_send()

            @pl.when((outer + 1 < self.lines) & (block <= outer))
            def _():
                self.pass_up(block).wait_send()

            @pl.when((outer > 0) & (block >= outer))
            def _():
                self.pass_down(block).wait_send()


def front_kernel(
    lines, slots, att_ref, res_ref, gain_ref, sel_ref, cot_ref, hidden_ref, norm_ref, rows_ref, cots_ref,
    att_all, send_sems, recv_sems, att_send, att_recv,
):
    me, sect = lax.axis_index("dp"), lax.axis_index("sect")
    outer, inner = me // 2, me % 2
    width = att_ref.shape[1]
    peers = [(me, lax.rem(sect + k, slots), None) for k in range(1, slots)]
    peers.append((outer * 2 + 1 - inner, sect, None))
    peers.append((jnp.minimum(outer + 1, lines - 1) * 2 + inner, sect, outer + 1 < lines))
    peers.append((jnp.maximum(outer - 1, 0) * 2 + inner, sect, outer > 0))
    sel = sel_ref[...]
    cots_ref[me] = jnp.dot(sel, cot_ref[...], preferred_element_type=jnp.float32).astype(jnp.bfloat16)
    greet(peers)
    copies = []
    for k in range(1, slots):
        target = lax.rem(sect + k, slots)
        copies.append(
            remote(att_ref, att_all.at[sect], att_send.at[k], att_recv.at[sect], me, target)
        )
        copies[-1].start()
    cots = LineGather(cots_ref, (send_sems, recv_sems), lines, 0)
    rows = LineGather(rows_ref, (send_sems, recv_sems), lines, 1)
    cots.start()
    att_all[sect] = att_ref[...]
    for k in range(1, slots):
        source = lax.rem(sect + k, slots)
        remote(att_ref, att_all.at[source], att_send.at[k], att_recv.at[source], me, source).wait_recv()
    square = jnp.zeros((res_ref.shape[0], 1), jnp.float32)
    for block in range(slots):
        cols = slice(block * width, (block + 1) * width)
        hid = (
            res_ref[:, cols].astype(jnp.float32) + att_all[block].astype(jnp.float32)
        ).astype(jnp.bfloat16)
        hidden_ref[:, cols] = hid
        hid_f = hid.astype(jnp.float32)
        square = square + jnp.sum(hid_f * hid_f, axis=-1, keepdims=True)
    inverse = lax.rsqrt(square / (slots * width) + 1e-05)
    norm_ref[...] = jnp.broadcast_to(inverse, norm_ref.shape)
    for block in range(slots):
        cols = slice(block * width, (block + 1) * width)
        normed = (hidden_ref[:, cols].astype(jnp.float32) * inverse * gain_ref[:, cols]).astype(
            jnp.bfloat16
        )
        rows_ref[me, :, cols] = jnp.dot(sel, normed, preferred_element_type=jnp.float32).astype(
            jnp.bfloat16
        )
    rows.start()
    for step in range(1, lines):
        cots.relay(step)
        rows.relay(step)
    cots.finish()
    rows.finish()
    for one in copies:
        one.wait_send()


def front(att, residual, gain_rows, selector, cotangent, dp, slots):
    length, width = residual.shape
    capacity = selector.shape[0]
    vm = pl.BlockSpec(memory_space=pltpu.VMEM)
    return pl.pallas_call(
        functools.partial(front_kernel, dp // 2, slots),
        out_shape=(
            jax.ShapeDtypeStruct((length, width), jnp.bfloat16),
            jax.ShapeDtypeStruct((length, 128), jnp.float32),
            jax.ShapeDtypeStruct((dp, capacity, width), jnp.bfloat16),
            jax.ShapeDtypeStruct((dp, capacity, width), jnp.bfloat16),
        ),
        in_specs=[vm] * 5,
        out_specs=(vm,) * 4,
        scratch_shapes=[
            pltpu.VMEM((slots,) + att.shape, jnp.bfloat16),
            pltpu.SemaphoreType.DMA((2, 3, dp // 2)),
            pltpu.SemaphoreType.DMA((2, 2, dp // 2)),
            pltpu.SemaphoreType.DMA((slots,)),
            pltpu.SemaphoreType.DMA((slots,)),
        ],
        compiler_params=pltpu.CompilerParams(
            collective_id=0, has_side_effects=True, vmem_limit_bytes=VMEM_BYTES
        ),
    )(att, residual, gain_rows, selector, cotangent)


def ffn_kernel(tail, rows_ref, cots_ref, up_ref, down_ref, out_ref, back_ref, upg_ref, downg_ref, out_acc, back_acc):
    step = pl.program_id(0)
    last = pl.num_programs(0) - 1
    full = up_ref.shape[0]

    @pl.when(step == 0)
    def _():
        out_acc[...] = jnp.zeros_like(out_acc)
        back_acc[...] = jnp.zeros_like(back_acc)

    def run(size):
        rows, cots = rows_ref[...], cots_ref[...]
        preact = contract_last(rows, up_ref[:size, :])
        back = contract_last(cots, down_ref[:size, :])
        sigma = jax.nn.sigmoid(preact)
        activated = (preact * sigma).astype(jnp.bfloat16)
        pre_grad = (back * sigma * (1.0 + preact * (1.0 - sigma))).astype(jnp.bfloat16)
        out_acc[...] += jnp.dot(activated, down_ref[:size, :], preferred_element_type=jnp.float32)
        back_acc[...] += jnp.dot(pre_grad, up_ref[:size, :], preferred_element_type=jnp.float32)
        downg_ref[:size, :] = contract_first(activated, cots).astype(jnp.bfloat16)
        upg_ref[:size, :] = contract_first(pre_grad, rows).astype(jnp.bfloat16)

    if tail == full:
        run(full)
    else:

        @pl.when(step < last)
        def _():
            run(full)

        @pl.when(step == last)
        def _():
            run(tail)

    @pl.when(step == last)
    def _():
        out_ref[...] = out_acc[...].astype(jnp.bfloat16)
        back_ref[...] = back_acc[...].astype(jnp.bfloat16)


def ffn(rows, cots, up, down):
    count, width = rows.shape
    hidden_units = up.shape[0]
    chunk = min(256 if count <= 128 else 128, hidden_units)
    steps = pl.cdiv(hidden_units, chunk)
    tail = hidden_units - (steps - 1) * chunk
    whole = pl.BlockSpec((count, width), lambda i: (0, 0))
    weight = pl.BlockSpec((chunk, width), lambda i: (i, 0))
    return pl.pallas_call(
        functools.partial(ffn_kernel, tail),
        grid=(steps,),
        out_shape=(
            jax.ShapeDtypeStruct((count, width), jnp.bfloat16),
            jax.ShapeDtypeStruct((count, width), jnp.bfloat16),
            jax.ShapeDtypeStruct(up.shape, jnp.bfloat16),
            jax.ShapeDtypeStruct(down.shape, jnp.bfloat16),
        ),
        in_specs=[whole, whole, weight, weight],
        out_specs=(whole, whole, weight, weight),
        scratch_shapes=[
            pltpu.VMEM((count, width), jnp.float32),
            pltpu.VMEM((count, width), jnp.float32),
        ],
        compiler_params=pltpu.CompilerParams(
            dimension_semantics=("arbitrary",), vmem_limit_bytes=VMEM_BYTES
        ),
    )(rows, cots, up, down)


def reduce_kernel(lines, slots, out_in, back_in, sums_ref, from_pair, pair_sum, from_line, pair_send, pair_recv,
                  line_send, line_recv, sect_send, sect_recv):
    me, sect = lax.axis_index("dp"), lax.axis_index("sect")
    outer, inner = me // 2, me % 2
    partner = outer * 2 + 1 - inner
    terms = (back_in, out_in)
    peers = [(me, lax.rem(sect + k, slots), None) for k in range(1, slots)]
    peers.append((partner, sect, None))
    for k in range(1, lines):
        peers.append((lax.rem(outer + k, lines) * 2 + inner, sect, None))
    greet(peers)
    order = [(k, step) for k in range(2) for step in list(range(1, lines)) + [0]]

    def across(k, step):
        line = lax.rem(outer + step, lines)
        return remote(
            terms[k].at[line * 2 + 1 - inner],
            from_pair.at[k, step],
            pair_send.at[k, step],
            pair_recv.at[k, step],
            partner,
            sect,
        )

    def along(k, step):
        line = lax.rem(outer + step, lines)
        return remote(
            pair_sum.at[k, step],
            from_line.at[k, step],
            line_send.at[k, step],
            line_recv.at[k, step],
            line * 2 + inner,
            sect,
        )

    def to_sect(k, hop):
        target = lax.rem(sect + hop, slots)
        return remote(
            sums_ref.at[k, sect],
            sums_ref.at[k, sect],
            sect_send.at[k, hop],
            sect_recv.at[k, sect],
            me,
            target,
        )

    def from_sect(k, hop):
        source = lax.rem(sect + hop, slots)
        return remote(
            sums_ref.at[k, source],
            sums_ref.at[k, source],
            sect_send.at[k, hop],
            sect_recv.at[k, source],
            me,
            source,
        )

    for k, step in order:
        across(k, step).start()
    for k in range(2):
        for step in list(range(1, lines)) + [0]:
            across(k, step).wait_recv()
            line = lax.rem(outer + step, lines)
            own = terms[k][line * 2 + inner].astype(jnp.float32) + from_pair[k, step].astype(jnp.float32)
            if step:
                pair_sum[k, step] = own.astype(jnp.bfloat16)
                along(k, step).start()
        for step in range(1, lines):
            along(k, step).wait_recv()
            own = own + from_line[k, step].astype(jnp.float32)
        sums_ref[k, sect] = own.astype(jnp.bfloat16)
        for hop in range(1, slots):
            to_sect(k, hop).start()
    for k in range(2):
        for hop in range(1, slots):
            from_sect(k, hop).wait_recv()
            to_sect(k, hop).wait_send()
        for step in range(lines):
            across(k, step).wait_send()
            if step:
                along(k, step).wait_send()


def reduce_terms(out_terms, back_terms, slots):
    dp, capacity, width = out_terms.shape
    lines = dp // 2
    vm = pl.BlockSpec(memory_space=pltpu.VMEM)
    dma = pltpu.SemaphoreType.DMA
    return pl.pallas_call(
        functools.partial(reduce_kernel, lines, slots),
        out_shape=jax.ShapeDtypeStruct((2, slots, capacity, width), jnp.bfloat16),
        in_specs=[vm] * 2,
        out_specs=vm,
        scratch_shapes=[
            pltpu.VMEM((2, lines, capacity, width), jnp.bfloat16),
            pltpu.VMEM((2, lines, capacity, width), jnp.bfloat16),
            pltpu.VMEM((2, lines, capacity, width), jnp.bfloat16),
            dma((2, lines)),
            dma((2, lines)),
            dma((2, lines)),
            dma((2, lines)),
            dma((2, slots)),
            dma((2, slots)),
        ],
        compiler_params=pltpu.CompilerParams(
            collective_id=1, has_side_effects=True, vmem_limit_bytes=VMEM_BYTES
        ),
    )(out_terms, back_terms)


def gain_kernel(dp, slots, part_ref, total_ref, inbox, mine, first_send, first_recv, next_send, next_recv, sect_send, sect_recv):
    me, sect = lax.axis_index("dp"), lax.axis_index("sect")
    peers = [(me, lax.rem(sect + k, slots), None) for k in range(1, slots)]
    peers += [(lax.rem(me + k, dp), sect, None) for k in range(1, dp)]
    greet(peers)

    def scatter(k):
        target = lax.rem(me + k, dp)
        return remote(
            part_ref.at[sect, target], inbox.at[k], first_send.at[k], first_recv.at[k], target, sect
        )

    def spread_sum(k):
        target = lax.rem(me + k, dp)
        return remote(
            mine, total_ref.at[sect, me], next_send.at[k], next_recv.at[k], target, sect
        )

    def to_sect(k):
        return remote(
            total_ref.at[sect],
            total_ref.at[sect],
            sect_send.at[k],
            sect_recv.at[k],
            me,
            lax.rem(sect + k, slots),
        )

    for k in range(1, dp):
        scatter(k).start()
    total = part_ref[sect, me]
    for k in range(1, dp):
        scatter(k).wait_recv()
        total = total + inbox[k]
    mine[...] = total
    for k in range(1, dp):
        spread_sum(k).start()
    total_ref[sect, me] = total
    for k in range(1, dp):
        spread_sum(k).wait_recv()
    for k in range(1, slots):
        to_sect(k).start()
    for k in range(1, slots):
        to_sect(k).wait_recv()
        to_sect(k).wait_send()
    for k in range(1, dp):
        scatter(k).wait_send()
        spread_sum(k).wait_send()


def gain_sum(part, dp, slots):
    kinds, width = part.shape
    cols = width // (dp * slots)
    padded = jnp.concatenate([part, jnp.zeros((8 - kinds, width), part.dtype)], 0)
    pieces = padded.reshape(8, slots, dp, cols).transpose(1, 2, 0, 3)
    vm = pl.BlockSpec(memory_space=pltpu.VMEM)
    dma = pltpu.SemaphoreType.DMA
    total = pl.pallas_call(
        functools.partial(gain_kernel, dp, slots),
        out_shape=jax.ShapeDtypeStruct(pieces.shape, pieces.dtype),
        in_specs=[vm],
        out_specs=vm,
        scratch_shapes=[
            pltpu.VMEM((dp, 8, cols), pieces.dtype),
            pltpu.VMEM((8, cols), pieces.dtype),
            dma((dp,)),
            dma((dp,)),
            dma((dp,)),
            dma((dp,)),
            dma((slots,)),
            dma((slots,)),
        ],
        compiler_params=pltpu.CompilerParams(collective_id=2, has_side_effects=True),
    )(pieces)
    return total.transpose(2, 0, 1, 3).reshape(8, width)[:kinds]


def contract_last(left, right):
    return lax.dot_general(
        left, right, (((1,), (1,)), ((), ())), preferred_element_type=jnp.float32
    )


def contract_first(left, right):
    return lax.dot_general(
        left, right, (((0,), (0,)), ((), ())), preferred_element_type=jnp.float32
    )


def selectors(token_labels, slot_modality):
    length = token_labels.shape[0]
    keep = token_labels[None, :] == slot_modality[:, None]
    rank = jnp.cumsum(keep.astype(jnp.int32), axis=1) - 1
    capacity = length // 2
    return (rank[:, None, :] == jnp.arange(capacity)[None, :, None]) & keep[:, None, :]


def on_device(
    dp, slots, queries, keys, values, residual, labels, slot_modality, gains, up_weight, down_weight, cotangent
):
    attended_block, probs, probs_b = causal_forward(queries, keys, values)
    token_labels = labels[0]
    onehot = (token_labels[:, None] == jnp.arange(MODALITIES)[None, :]).astype(jnp.float32)
    gain_rows = jnp.dot(onehot, gains, precision=lax.Precision.HIGHEST)
    slot_index = lax.axis_index("sect")
    all_select = selectors(token_labels, slot_modality).astype(jnp.bfloat16)
    selector = lax.dynamic_index_in_dim(all_select, slot_index, 0, keepdims=False)
    capacity, length = selector.shape
    grad_full = cotangent[0]
    hidden, inverse, rows, cots = front(
        attended_block[0], residual[0], gain_rows, selector, grad_full, dp, slots
    )
    width = hidden.shape[1]
    inverse = inverse[:, :1]
    hidden_f = hidden.astype(jnp.float32)
    normed_f = hidden_f * inverse
    out_terms, back_terms, up_grad, down_grad = ffn(
        rows.reshape(-1, width), cots.reshape(-1, width), up_weight[0], down_weight[0]
    )
    sums = reduce_terms(
        out_terms.reshape(dp, capacity, width), back_terms.reshape(dp, capacity, width), slots
    ).reshape(2, slots * capacity, width)
    place = all_select.reshape(slots * capacity, length)
    norm_grad = contract_first(place, sums[0])
    quarter = length // slots
    place_own = lax.dynamic_slice_in_dim(place, slot_index * quarter, quarter, 1)
    hidden_own = lax.dynamic_slice_in_dim(hidden_f, slot_index * quarter, quarter, 0)
    output = (hidden_own + contract_first(place_own, sums[1])).astype(jnp.bfloat16)[None]
    scaled = norm_grad * gain_rows
    hidden_grad = grad_full.astype(jnp.float32) + inverse * (
        scaled - normed_f * jnp.mean(scaled * normed_f, axis=-1, keepdims=True)
    )
    residual_full = hidden_grad.astype(jnp.bfloat16)
    residual_grad = lax.dynamic_slice_in_dim(residual_full, slot_index * quarter, quarter, 0)[None]
    gain_part = jnp.dot(onehot.T, norm_grad * normed_f, precision=lax.Precision.HIGHEST)
    gain_grad = gain_sum(gain_part, dp, slots)
    block_width = queries.shape[2]
    grad_block = lax.dynamic_slice_in_dim(residual_full, slot_index * block_width, block_width, 1)[
        None
    ]
    query_grad, key_grad, value_grad = causal_backward(
        grad_block, queries, keys, values, attended_block, probs, probs_b
    )
    return (
        output, residual_grad, query_grad, key_grad, value_grad, up_grad[None], down_grad[None], gain_grad,
    )


def solution(mesh):
    in_specs = (
        P("dp", None, "sect"),
        P("dp", None, "sect"),
        P("dp", None, "sect"),
        P("dp", None, None),
        P("dp", None),
        P(),
        P(),
        P("sect", "dp", None),
        P("sect", "dp", None),
        P("dp", None, None),
    )
    out_specs = (
        P("dp", "sect", None),
        P("dp", "sect", None),
        P("dp", None, "sect"),
        P("dp", None, "sect"),
        P("dp", None, "sect"),
        P("sect", "dp", None),
        P("sect", "dp", None),
        P(),
    )
    body = functools.partial(on_device, mesh.shape["dp"], mesh.shape["sect"])
    return jax.shard_map(
        body, mesh=mesh, in_specs=in_specs, out_specs=out_specs, check_vma=False
    )
```

```python
import functools

import jax
import jax.numpy as jnp
from jax import lax
from jax.experimental import pallas as pl
from jax.experimental.pallas import tpu as pltpu
from jax.sharding import PartitionSpec as P

HD = 128
MODALITIES = 3


def causal_forward(queries, keys, values):
    seq_count, length, width = queries.shape
    head_count = width // HD
    query_f = queries.astype(jnp.float32).reshape(seq_count, length, head_count, HD)
    key_f = keys.astype(jnp.float32).reshape(seq_count, length, head_count, HD)
    value_f = values.astype(jnp.float32).reshape(seq_count, length, head_count, HD)
    scores = jnp.einsum("sqhd,skhd->shqk", query_f, key_f) * HD ** (-0.5)
    position = jnp.arange(length)
    causal = position[:, None] >= position[None, :]
    scores = jnp.where(causal, scores, -1e30)
    probs = jax.nn.softmax(scores, axis=-1)
    probs_b = probs.astype(jnp.bfloat16)
    attended = jnp.einsum("shqk,skhd->sqhd", probs_b.astype(jnp.float32), value_f)
    return (attended.astype(jnp.bfloat16).reshape(seq_count, length, width), probs, probs_b)


MESH = pl.DeviceIdType.MESH
VMEM_BYTES = 60 * 1024 * 1024


def remote(src, dst, send_sem, recv_sem, dp_index, sect_index):
    return pltpu.make_async_remote_copy(
        src_ref=src,
        dst_ref=dst,
        send_sem=send_sem,
        recv_sem=recv_sem,
        device_id=(dp_index, sect_index),
        device_id_type=MESH,
    )


def greet(peers):
    barrier = pltpu.get_barrier_semaphore()
    total = jnp.int32(0)
    for dp_index, sect_index, present in peers:
        if present is None:
            pl.semaphore_signal(barrier, inc=1, device_id=(dp_index, sect_index), device_id_type=MESH)
            total = total + 1
        else:

            @pl.when(present)
            def _():
                pl.semaphore_signal(
                    barrier, inc=1, device_id=(dp_index, sect_index), device_id_type=MESH
                )

            total = total + present.astype(jnp.int32)
    pl.semaphore_wait(barrier, total)


class LineGather:
    def __init__(self, buf, sems, lines, slot):
        self.buf, self.lines = buf, lines
        self.send_sems, self.recv_sems = sems
        self.slot = slot
        self.me = lax.axis_index("dp")
        self.sect = lax.axis_index("sect")
        self.outer, self.inner = self.me // 2, self.me % 2

    def copy(self, way, outer, target, incoming=False):
        inner = (1 - self.inner) if (incoming and way == 2) else self.inner
        block = self.buf.at[outer * 2 + inner]
        recv = 1 if way == 2 else 0
        return remote(
            block,
            block,
            self.send_sems.at[self.slot, way, outer],
            self.recv_sems.at[self.slot, recv, outer],
            target,
            self.sect,
        )

    def pass_up(self, outer):
        return self.copy(0, outer, jnp.minimum(self.outer + 1, self.lines - 1) * 2 + self.inner)

    def pass_down(self, outer):
        return self.copy(1, outer, jnp.maximum(self.outer - 1, 0) * 2 + self.inner)

    def pass_across(self, outer):
        return self.copy(2, outer, self.outer * 2 + 1 - self.inner)

    def start(self):
        outer = self.outer

        @pl.when(outer + 1 < self.lines)
        def _():
            self.pass_up(outer).start()

        @pl.when(outer > 0)
        def _():
            self.pass_down(outer).start()

        self.pass_across(outer).start()

    def relay(self, step):
        outer = self.outer

        @pl.when(outer - step >= 0)
        def _():
            block = outer - step
            self.pass_down(block).wait_recv()

            @pl.when(outer + 1 < self.lines)
            def _():
                self.pass_up(block).start()

            self.pass_across(block).start()

        @pl.when(outer + step < self.lines)
        def _():
            block = outer + step
            self.pass_up(block).wait_recv()

            @pl.when(outer > 0)
            def _():
                self.pass_down(block).start()

            self.pass_across(block).start()

    def finish(self):
        outer = self.outer
        for block in range(self.lines):
            self.copy(2, block, self.outer * 2 + 1 - self.inner, incoming=True).wait_recv()
            self.pass_across(block).wait_send()

            @pl.when((outer + 1 < self.lines) & (block <= outer))
            def _():
                self.pass_up(block).wait_send()

            @pl.when((outer > 0) & (block >= outer))
            def _():
                self.pass_down(block).wait_send()


def front_kernel(
    lines, slots, att_ref, res_ref, gain_ref, sel_ref, cot_ref, hidden_ref, norm_ref, rows_ref, cots_ref,
    att_all, send_sems, recv_sems, att_send, att_recv,
):
    me, sect = lax.axis_index("dp"), lax.axis_index("sect")
    outer, inner = me // 2, me % 2
    width = att_ref.shape[1]
    peers = [(me, lax.rem(sect + k, slots), None) for k in range(1, slots)]
    peers.append((outer * 2 + 1 - inner, sect, None))
    peers.append((jnp.minimum(outer + 1, lines - 1) * 2 + inner, sect, outer + 1 < lines))
    peers.append((jnp.maximum(outer - 1, 0) * 2 + inner, sect, outer > 0))
    sel = sel_ref[...]
    cots_ref[me] = jnp.dot(sel, cot_ref[...], preferred_element_type=jnp.float32).astype(jnp.bfloat16)
    greet(peers)
    copies = []
    for k in range(1, slots):
        target = lax.rem(sect + k, slots)
        copies.append(
            remote(att_ref, att_all.at[sect], att_send.at[k], att_recv.at[sect], me, target)
        )
        copies[-1].start()
    cots = LineGather(cots_ref, (send_sems, recv_sems), lines, 0)
    rows = LineGather(rows_ref, (send_sems, recv_sems), lines, 1)
    cots.start()
    att_all[sect] = att_ref[...]
    for k in range(1, slots):
        source = lax.rem(sect + k, slots)
        remote(att_ref, att_all.at[source], att_send.at[k], att_recv.at[source], me, source).wait_recv()
    square = jnp.zeros((res_ref.shape[0], 1), jnp.float32)
    for block in range(slots):
        cols = slice(block * width, (block + 1) * width)
        hid = (
            res_ref[:, cols].astype(jnp.float32) + att_all[block].astype(jnp.float32)
        ).astype(jnp.bfloat16)
        hidden_ref[:, cols] = hid
        hid_f = hid.astype(jnp.float32)
        square = square + jnp.sum(hid_f * hid_f, axis=-1, keepdims=True)
    inverse = lax.rsqrt(square / (slots * width) + 1e-05)
    norm_ref[...] = jnp.broadcast_to(inverse, norm_ref.shape)
    for block in range(slots):
        cols = slice(block * width, (block + 1) * width)
        normed = (hidden_ref[:, cols].astype(jnp.float32) * inverse * gain_ref[:, cols]).astype(
            jnp.bfloat16
        )
        rows_ref[me, :, cols] = jnp.dot(sel, normed, preferred_element_type=jnp.float32).astype(
            jnp.bfloat16
        )
    rows.start()
    for step in range(1, lines):
        cots.relay(step)
        rows.relay(step)
    cots.finish()
    rows.finish()
    for one in copies:
        one.wait_send()


def front(att, residual, gain_rows, selector, cotangent, dp, slots):
    length, width = residual.shape
    capacity = selector.shape[0]
    vm = pl.BlockSpec(memory_space=pltpu.VMEM)
    return pl.pallas_call(
        functools.partial(front_kernel, dp // 2, slots),
        out_shape=(
            jax.ShapeDtypeStruct((length, width), jnp.bfloat16),
            jax.ShapeDtypeStruct((length, 128), jnp.float32),
            jax.ShapeDtypeStruct((dp, capacity, width), jnp.bfloat16),
            jax.ShapeDtypeStruct((dp, capacity, width), jnp.bfloat16),
        ),
        in_specs=[vm] * 5,
        out_specs=(vm,) * 4,
        scratch_shapes=[
            pltpu.VMEM((slots,) + att.shape, jnp.bfloat16),
            pltpu.SemaphoreType.DMA((2, 3, dp // 2)),
            pltpu.SemaphoreType.DMA((2, 2, dp // 2)),
            pltpu.SemaphoreType.DMA((slots,)),
            pltpu.SemaphoreType.DMA((slots,)),
        ],
        compiler_params=pltpu.CompilerParams(
            collective_id=0, has_side_effects=True, vmem_limit_bytes=VMEM_BYTES
        ),
    )(att, residual, gain_rows, selector, cotangent)


def ffn_kernel(tail, rows_ref, cots_ref, up_ref, down_ref, out_ref, back_ref, upg_ref, downg_ref, out_acc, back_acc):
    step = pl.program_id(0)
    last = pl.num_programs(0) - 1
    full = up_ref.shape[0]

    @pl.when(step == 0)
    def _():
        out_acc[...] = jnp.zeros_like(out_acc)
        back_acc[...] = jnp.zeros_like(back_acc)

    def run(size):
        rows, cots = rows_ref[...], cots_ref[...]
        preact = contract_last(rows, up_ref[:size, :])
        back = contract_last(cots, down_ref[:size, :])
        sigma = jax.nn.sigmoid(preact)
        activated = (preact * sigma).astype(jnp.bfloat16)
        pre_grad = (back * sigma * (1.0 + preact * (1.0 - sigma))).astype(jnp.bfloat16)
        out_acc[...] += jnp.dot(activated, down_ref[:size, :], preferred_element_type=jnp.float32)
        back_acc[...] += jnp.dot(pre_grad, up_ref[:size, :], preferred_element_type=jnp.float32)
        downg_ref[:size, :] = contract_first(activated, cots).astype(jnp.bfloat16)
        upg_ref[:size, :] = contract_first(pre_grad, rows).astype(jnp.bfloat16)

    if tail == full:
        run(full)
    else:

        @pl.when(step < last)
        def _():
            run(full)

        @pl.when(step == last)
        def _():
            run(tail)

    @pl.when(step == last)
    def _():
        out_ref[...] = out_acc[...].astype(jnp.bfloat16)
        back_ref[...] = back_acc[...].astype(jnp.bfloat16)


def ffn(rows, cots, up, down):
    count, width = rows.shape
    hidden_units = up.shape[0]
    chunk = min(256 if count <= 128 else 128, hidden_units)
    steps = pl.cdiv(hidden_units, chunk)
    tail = hidden_units - (steps - 1) * chunk
    whole = pl.BlockSpec((count, width), lambda i: (0, 0))
    weight = pl.BlockSpec((chunk, width), lambda i: (i, 0))
    return pl.pallas_call(
        functools.partial(ffn_kernel, tail),
        grid=(steps,),
        out_shape=(
            jax.ShapeDtypeStruct((count, width), jnp.bfloat16),
            jax.ShapeDtypeStruct((count, width), jnp.bfloat16),
            jax.ShapeDtypeStruct(up.shape, jnp.bfloat16),
            jax.ShapeDtypeStruct(down.shape, jnp.bfloat16),
        ),
        in_specs=[whole, whole, weight, weight],
        out_specs=(whole, whole, weight, weight),
        scratch_shapes=[
            pltpu.VMEM((count, width), jnp.float32),
            pltpu.VMEM((count, width), jnp.float32),
        ],
        compiler_params=pltpu.CompilerParams(
            dimension_semantics=("arbitrary",), vmem_limit_bytes=VMEM_BYTES
        ),
    )(rows, cots, up, down)


def reduce_kernel(lines, slots, out_in, back_in, norm_sums, out_sums, from_pair, pair_sum, from_line, pair_send, pair_recv,
                  line_send, line_recv, sect_send, sect_recv):
    me, sect = lax.axis_index("dp"), lax.axis_index("sect")
    outer, inner = me // 2, me % 2
    partner = outer * 2 + 1 - inner
    terms = (back_in, out_in)
    peers = [(me, lax.rem(sect + k, slots), None) for k in range(1, slots)]
    peers.append((partner, sect, None))
    for k in range(1, lines):
        peers.append((lax.rem(outer + k, lines) * 2 + inner, sect, None))
    greet(peers)
    order = [(k, step) for k in range(2) for step in list(range(1, lines)) + [0]]

    def across(k, step):
        line = lax.rem(outer + step, lines)
        return remote(
            terms[k].at[line * 2 + 1 - inner],
            from_pair.at[k, step],
            pair_send.at[k, step],
            pair_recv.at[k, step],
            partner,
            sect,
        )

    def along(k, step):
        line = lax.rem(outer + step, lines)
        return remote(
            pair_sum.at[k, step],
            from_line.at[k, step],
            line_send.at[k, step],
            line_recv.at[k, step],
            line * 2 + inner,
            sect,
        )

    sums = (norm_sums, out_sums)
    near = sect + 1 - 2 * (sect % 2)
    far = lax.rem(sect + 2, slots)
    far_near = lax.rem(near + 2, slots)

    def hand(k, way, block, target):
        return remote(
            sums[k].at[block], sums[k].at[block], sect_send.at[k, way], sect_recv.at[k, block], me, target
        )

    for k, step in order:
        across(k, step).start()
    for k in range(2):
        for step in list(range(1, lines)) + [0]:
            across(k, step).wait_recv()
            line = lax.rem(outer + step, lines)
            own = terms[k][line * 2 + inner].astype(jnp.float32) + from_pair[k, step].astype(jnp.float32)
            if step:
                pair_sum[k, step] = own.astype(jnp.bfloat16)
                along(k, step).start()
        for step in range(1, lines):
            along(k, step).wait_recv()
            own = own + from_line[k, step].astype(jnp.float32)
        sums[k][sect] = own.astype(sums[k].dtype)
        hand(k, 1, sect, far).start()
        hand(k, 0, sect, near).start()
    for k in range(2):
        hand(k, 1, far, far).wait_recv()
        hand(k, 2, far, near).start()
    for k in range(2):
        hand(k, 0, near, near).wait_recv()
        hand(k, 2, far_near, near).wait_recv()
        hand(k, 0, sect, near).wait_send()
        hand(k, 1, sect, far).wait_send()
        hand(k, 2, far, near).wait_send()
        for step in range(lines):
            across(k, step).wait_send()
            if step:
                along(k, step).wait_send()


def reduce_terms(out_terms, back_terms, slots):
    dp, capacity, width = out_terms.shape
    lines = dp // 2
    vm = pl.BlockSpec(memory_space=pltpu.VMEM)
    dma = pltpu.SemaphoreType.DMA
    return pl.pallas_call(
        functools.partial(reduce_kernel, lines, slots),
        out_shape=(
            jax.ShapeDtypeStruct((slots, capacity, width), jnp.float32),
            jax.ShapeDtypeStruct((slots, capacity, width), jnp.bfloat16),
        ),
        in_specs=[vm] * 2,
        out_specs=(vm, vm),
        scratch_shapes=[
            pltpu.VMEM((2, lines, capacity, width), jnp.bfloat16),
            pltpu.VMEM((2, lines, capacity, width), jnp.bfloat16),
            pltpu.VMEM((2, lines, capacity, width), jnp.bfloat16),
            dma((2, lines)),
            dma((2, lines)),
            dma((2, lines)),
            dma((2, lines)),
            dma((2, 3)),
            dma((2, slots)),
        ],
        compiler_params=pltpu.CompilerParams(
            collective_id=1, has_side_effects=True, vmem_limit_bytes=VMEM_BYTES
        ),
    )(out_terms, back_terms)


def head_grads(refs, heads):
    query_ref, key_ref, value_ref, att_ref, grad_ref, query_out, key_out, value_out = refs
    length = query_ref.shape[0]
    rows = lax.broadcasted_iota(jnp.int32, (length, length), 0)
    cols = lax.broadcasted_iota(jnp.int32, (length, length), 1)
    for head in heads:
        block = slice(head * HD, (head + 1) * HD)
        query, key, value, grad = (one[:, block] for one in (query_ref, key_ref, value_ref, grad_ref))
        scores = jnp.where(rows >= cols, contract_last(query, key) * HD ** (-0.5), -1e30)
        raised = jnp.exp(scores - jnp.max(scores, axis=-1, keepdims=True))
        probs = raised / jnp.sum(raised, axis=-1, keepdims=True)
        value_out[:, block] = contract_first(probs.astype(jnp.bfloat16), grad).astype(jnp.bfloat16)
        delta = jnp.sum(
            grad.astype(jnp.float32) * att_ref[:, block].astype(jnp.float32), axis=-1, keepdims=True
        )
        dscore = (probs * (contract_last(grad, value) - delta) * HD ** (-0.5)).astype(jnp.bfloat16)
        query_out[:, block] = jnp.dot(dscore, key, preferred_element_type=jnp.float32).astype(
            jnp.bfloat16
        )
        key_out[:, block] = contract_first(dscore, query).astype(jnp.bfloat16)


def gain_kernel(dp, slots, part_ref, query_ref, key_ref, value_ref, att_ref, grad_ref, total_ref, query_out, key_out, value_out, inbox, mine, first_send, first_recv, next_send, next_recv, sect_send, sect_recv):
    me, sect = lax.axis_index("dp"), lax.axis_index("sect")
    peers = [(me, lax.rem(sect + k, slots), None) for k in range(1, slots)]
    peers += [(lax.rem(me + k, dp), sect, None) for k in range(1, dp)]
    greet(peers)

    def scatter(k):
        target = lax.rem(me + k, dp)
        return remote(
            part_ref.at[sect, target], inbox.at[k], first_send.at[k], first_recv.at[k], target, sect
        )

    def spread_sum(k):
        target = lax.rem(me + k, dp)
        return remote(
            mine, total_ref.at[sect, me], next_send.at[k], next_recv.at[k], target, sect
        )

    def to_sect(k):
        return remote(
            total_ref.at[sect],
            total_ref.at[sect],
            sect_send.at[k],
            sect_recv.at[k],
            me,
            lax.rem(sect + k, slots),
        )

    for k in range(1, dp):
        scatter(k).start()
    refs = (query_ref, key_ref, value_ref, att_ref, grad_ref, query_out, key_out, value_out)
    head_count = query_ref.shape[1] // HD
    head_grads(refs, range(head_count // 2))
    total = part_ref[sect, me]
    for k in range(1, dp):
        scatter(k).wait_recv()
        total = total + inbox[k]
    mine[...] = total
    for k in range(1, dp):
        spread_sum(k).start()
    total_ref[sect, me] = total
    head_grads(refs, range(head_count // 2, head_count))
    for k in range(1, dp):
        spread_sum(k).wait_recv()
    for k in range(1, slots):
        to_sect(k).start()
    for k in range(1, slots):
        to_sect(k).wait_recv()
        to_sect(k).wait_send()
    for k in range(1, dp):
        scatter(k).wait_send()
        spread_sum(k).wait_send()


def gain_sum(part, queries, keys, values, attended, grad, dp, slots):
    kinds, width = part.shape
    cols = width // (dp * slots)
    padded = jnp.concatenate([part, jnp.zeros((8 - kinds, width), part.dtype)], 0)
    pieces = padded.reshape(8, slots, dp, cols).transpose(1, 2, 0, 3)
    vm = pl.BlockSpec(memory_space=pltpu.VMEM)
    dma = pltpu.SemaphoreType.DMA
    like = jax.ShapeDtypeStruct(queries.shape, queries.dtype)
    total, *grads = pl.pallas_call(
        functools.partial(gain_kernel, dp, slots),
        out_shape=(jax.ShapeDtypeStruct(pieces.shape, pieces.dtype), like, like, like),
        in_specs=[vm] * 6,
        out_specs=(vm,) * 4,
        scratch_shapes=[
            pltpu.VMEM((dp, 8, cols), pieces.dtype),
            pltpu.VMEM((8, cols), pieces.dtype),
            dma((dp,)),
            dma((dp,)),
            dma((dp,)),
            dma((dp,)),
            dma((slots,)),
            dma((slots,)),
        ],
        compiler_params=pltpu.CompilerParams(collective_id=2, has_side_effects=True),
    )(pieces, queries, keys, values, attended, grad)
    return total.transpose(2, 0, 1, 3).reshape(8, width)[:kinds], grads


def contract_last(left, right):
    return lax.dot_general(
        left, right, (((1,), (1,)), ((), ())), preferred_element_type=jnp.float32
    )


def contract_first(left, right):
    return lax.dot_general(
        left, right, (((0,), (0,)), ((), ())), preferred_element_type=jnp.float32
    )


def selectors(token_labels, slot_modality):
    length = token_labels.shape[0]
    keep = token_labels[None, :] == slot_modality[:, None]
    rank = jnp.cumsum(keep.astype(jnp.int32), axis=1) - 1
    capacity = length // 2
    return (rank[:, None, :] == jnp.arange(capacity)[None, :, None]) & keep[:, None, :]


def on_device(
    dp, slots, queries, keys, values, residual, labels, slot_modality, gains, up_weight, down_weight, cotangent
):
    attended_block, probs, probs_b = causal_forward(queries, keys, values)
    token_labels = labels[0]
    onehot = (token_labels[:, None] == jnp.arange(MODALITIES)[None, :]).astype(jnp.float32)
    gain_rows = jnp.dot(onehot, gains, precision=lax.Precision.HIGHEST)
    slot_index = lax.axis_index("sect")
    all_select = selectors(token_labels, slot_modality).astype(jnp.bfloat16)
    selector = lax.dynamic_index_in_dim(all_select, slot_index, 0, keepdims=False)
    capacity, length = selector.shape
    grad_full = cotangent[0]
    hidden, inverse, rows, cots = front(
        attended_block[0], residual[0], gain_rows, selector, grad_full, dp, slots
    )
    width = hidden.shape[1]
    inverse = inverse[:, :1]
    hidden_f = hidden.astype(jnp.float32)
    normed_f = hidden_f * inverse
    out_terms, back_terms, up_grad, down_grad = ffn(
        rows.reshape(-1, width), cots.reshape(-1, width), up_weight[0], down_weight[0]
    )
    norm_sums, out_sums = reduce_terms(
        out_terms.reshape(dp, capacity, width), back_terms.reshape(dp, capacity, width), slots
    )
    place = all_select.reshape(slots * capacity, length)
    norm_grad = lax.dot_general(
        place.astype(jnp.float32),
        norm_sums.reshape(slots * capacity, width),
        (((0,), (0,)), ((), ())),
        precision=lax.Precision.HIGHEST,
    )
    quarter = length // slots
    place_own = lax.dynamic_slice_in_dim(place, slot_index * quarter, quarter, 1)
    hidden_own = lax.dynamic_slice_in_dim(hidden_f, slot_index * quarter, quarter, 0)
    output = (hidden_own + contract_first(place_own, out_sums.reshape(slots * capacity, width))).astype(jnp.bfloat16)[None]
    scaled = norm_grad * gain_rows
    hidden_grad = grad_full.astype(jnp.float32) + inverse * (
        scaled - normed_f * jnp.mean(scaled * normed_f, axis=-1, keepdims=True)
    )
    residual_full = hidden_grad.astype(jnp.bfloat16)
    residual_grad = lax.dynamic_slice_in_dim(residual_full, slot_index * quarter, quarter, 0)[None]
    gain_part = jnp.dot(onehot.T, norm_grad * normed_f, precision=lax.Precision.HIGHEST)
    block_width = queries.shape[2]
    grad_block = lax.dynamic_slice_in_dim(residual_full, slot_index * block_width, block_width, 1)
    gain_grad, (query_grad, key_grad, value_grad) = gain_sum(
        gain_part, queries[0], keys[0], values[0], attended_block[0], grad_block, dp, slots
    )
    return (
        output, residual_grad, query_grad[None], key_grad[None], value_grad[None], up_grad[None], down_grad[None], gain_grad,
    )


def solution(mesh):
    in_specs = (
        P("dp", None, "sect"),
        P("dp", None, "sect"),
        P("dp", None, "sect"),
        P("dp", None, None),
        P("dp", None),
        P(),
        P(),
        P("sect", "dp", None),
        P("sect", "dp", None),
        P("dp", None, None),
    )
    out_specs = (
        P("dp", "sect", None),
        P("dp", "sect", None),
        P("dp", None, "sect"),
        P("dp", None, "sect"),
        P("dp", None, "sect"),
        P("sect", "dp", None),
        P("sect", "dp", None),
        P(),
    )
    body = functools.partial(on_device, mesh.shape["dp"], mesh.shape["sect"])
    return jax.shard_map(
        body, mesh=mesh, in_specs=in_specs, out_specs=out_specs, check_vma=False
    )
```
